128 devices in a mesh: test: 8 (over y, core), src: 16 (over z, x).
Axes of the slice: x: 4, y: 4, z: 4, core: 2. Of those that a mesh axis runs over, the one named last changes fastest.
Arguments:
- test_points: float32 [16, 3, 1024], P('test'), may hold values from 0 to 1
- test_basis: bfloat16 [16, 1024, 384], P('test'), may hold values from -0.1875 to 0.1875
- test_counts: int32 [16], P('test'), may hold values from 128 to 384, as said below
- source_points: float32 [128, 3, 1024], P('src'), may hold values from 0 to 1
- source_basis: bfloat16 [128, 1024, 384], P('src', 'test'), may hold values from -0.1875 to 0.1875
- source_counts: int32 [128], P('src'), may hold values from 128 to 384, as said below
- coefficients: bfloat16 [128, 384, 512], P('src'), may hold values from -0.0390625 to 0.0390625
Outputs:
- reduced: bfloat16 [16, 384, 128, 384], P('test', 'src')
- projected: bfloat16 [16, 384, 512], P('test', 'src')
The draws below stay inside these ranges and needn't reach their ends.
Inputs may be any that keep to these rules, and one draw needn't show every extreme that they name: `test_counts`: number of leading basis columns of a test block that are used; the rest are ignored. Some test block uses all 384 in every draw. `source_counts`: number of leading basis columns of a source block that are used; the rest are ignored. Some source block uses all 384 in every draw.
All inputs are finite; a program needn't handle non-finite values.
Results may differ from the reference program's by a relative error of at most 0.015.
Values may be sent and summed in bfloat16 or wider, within the bound.
A program may use at most 128 MiB of HBM per device.

```python
import jax
import jax.numpy as jnp
from jax import lax

B = 1024
KMAX = 384
NCOL = 512
NTB = 16
NSB = 128


def count_draw(key, length):
    counts = jax.random.randint(key, (length,), KMAX // 3, KMAX + 1)
    top_pos = jax.random.randint(jax.random.fold_in(key, 11), (), 0, length)
    low_pos = jax.random.randint(jax.random.fold_in(key, 12), (), 0, length)
    counts = counts.at[low_pos].set(KMAX // 3)
    counts = counts.at[top_pos].set(KMAX)
    return counts.astype(jnp.int32)


def draw_test_counts(key, part):
    return count_draw(jax.random.fold_in(key, 101), NTB)


def draw_source_counts(key, part):
    return count_draw(jax.random.fold_in(key, 202), NSB)


def shard_levels(rng, extent, cuts, low, high):
    factor_of, own = 1.0, jax.random.fold_in(rng, 6)
    for position, blocks in cuts:
        heights = jnp.exp(jax.random.uniform(jax.random.fold_in(own, position), (blocks,), jnp.float32, low / len(cuts), high / len(cuts)))
        factor_of = factor_of * jnp.repeat(heights, extent[position] // blocks).reshape([-1 if axis == position else 1 for axis in range(len(extent))])
    return factor_of


def noise(stream_key, shape, deviation, most, cuts=(), held_as=jnp.bfloat16):
    drawn = jax.random.normal(stream_key, shape, jnp.float32) * deviation
    if len(cuts) > 0:
        drawn = shard_levels(stream_key, shape, cuts, -0.22, 0.18) * drawn
    return jnp.clip(drawn, min=-most, max=most).astype(held_as)


def setup_inputs(seed: int = 0) -> dict:
    seeds = jax.random.split(jax.random.key(seed), 8)
    return {
        "test_points": jnp.clip(1.0 * jax.random.uniform(seeds[0], (NTB, 3, B), jnp.float32) ** shard_levels(seeds[0], (NTB, 3, B), ((0, 8),), -0.2, 0.2), 0.0, 1.0),
        "test_basis": noise(seeds[1], (NTB, B, KMAX), B ** -0.5, 0.1875, ((0, 8),)),
        "test_counts": draw_test_counts(jax.random.fold_in(seeds[7], 71), 0),
        "source_points": jnp.clip(1.0 * jax.random.uniform(seeds[3], (NSB, 3, B), jnp.float32) ** shard_levels(seeds[3], (NSB, 3, B), ((0, 16),), -0.2, 0.2), 0.0, 1.0),
        "source_basis": noise(seeds[4], (NSB, B, KMAX), B ** -0.5, 0.1875, ((0, 16), (1, 8))),
        "source_counts": draw_source_counts(jax.random.fold_in(seeds[7], 71), 0),
        "coefficients": noise(seeds[6], (NSB, KMAX, NCOL), (KMAX * NSB // 2) ** -0.5, 0.0390625, ((0, 16),)),
    }


softening = 0.0025

def tile_kernel(test_xyz, source_xyz):
    total = jnp.zeros((test_xyz.shape[1], source_xyz.shape[1]), test_xyz.dtype)
    for comp in range(3):
        delta = test_xyz[comp][:, None] - source_xyz[comp][None, :]
        total = total + delta * delta
    return lax.rsqrt(total + softening)

def reference(test_points, test_basis, test_counts, source_points, source_basis, source_counts, coefficients):
    column_ids = lax.iota(jnp.int32, KMAX)
    test_mask = (column_ids[None, None, :] < test_counts[:, None, None]).astype(jnp.bfloat16)
    source_mask = (column_ids[None, None, :] < source_counts[:, None, None]).astype(jnp.bfloat16)
    test_masked = test_basis * test_mask
    source_masked = source_basis * source_mask

    def per_test(inputs):
        test_xyz, test_side = inputs

        def per_source(carry, sinputs):
            source_xyz, source_side, coeff = sinputs
            kernel = tile_kernel(test_xyz, source_xyz).astype(jnp.bfloat16)
            half = jnp.dot(kernel, source_side, preferred_element_type=jnp.float32).astype(jnp.bfloat16)
            tile = lax.dot_general(test_side, half, (((0,), (0,)), ((), ())), preferred_element_type=jnp.float32).astype(jnp.bfloat16)
            carry = carry + jnp.dot(tile, coeff, preferred_element_type=jnp.float32)
            return (carry, tile)
        start = jnp.zeros((KMAX, NCOL), jnp.float32)
        total, tiles = lax.scan(per_source, start, (source_points, source_masked, coefficients))
        return (tiles, total.astype(jnp.bfloat16))
    tiles, projected = lax.map(per_test, (test_points, test_masked))
    reduced = jnp.transpose(tiles, (0, 2, 1, 3))
    return (reduced, projected)
```

```python
import functools

import jax
import jax.numpy as jnp
from jax import lax
from jax.experimental import pallas as pl
from jax.experimental.pallas import tpu as pltpu
from jax.sharding import PartitionSpec as P

softening = 0.0025
MESH = pl.DeviceIdType.MESH
RING = 4
LAG = 3
PARTS = ((0, 1), (1, 2))
AHEAD = 3
HOPS = [(1, 0), (0, 1), (3, 0), (0, 3), (2, 1), (1, 2), (2, 3), (3, 2), (1, 1), (3, 3), (1, 3), (3, 1), (2, 0), (0, 2), (2, 2)]
F32 = jnp.float32
BF16 = jnp.bfloat16


def fused(
    tc_hbm, sc_hbm, tp_hbm, sp_hbm, u_hbm, coeff_hbm, vown,
    mixed, pstage,
    stage, vbuf, tiles, acc, accb, part1, psum, kbuf, tcol, srow, half, tc_ref, sc_ref, tp, sp, u, ut, coeff,
    ssem, rsem, psend, precv, vsend, vdir, vpart, lsem, osem, sdir, spart,
):
    t = lax.axis_index("test")
    s = lax.axis_index("src")
    y, c = t // 2, t % 2
    z, x = s // RING, s % RING
    nj, chunk = vown.shape[0], vown.shape[1]
    ni, npts, kmax = u.shape
    nsrc, rows = stage.shape[0], stage.shape[4]
    nstrip = kmax // 128
    wide = npts // 128
    others = nsrc - 1

    def src_peer(hop):
        return ((z + hop[0]) % RING) * RING + (x + hop[1]) % RING

    partner = {"test": y * 2 + (1 - c)}
    ypeers = [{"test": ((y + d) % RING) * 2 + c} for d in (1, 3, 2)]

    barrier = pltpu.get_barrier_semaphore()
    for hop in HOPS:
        pl.semaphore_signal(barrier, inc=1, device_id={"src": src_peer(hop)}, device_id_type=MESH)
    for peer in [partner] + ypeers:
        pl.semaphore_signal(barrier, inc=1, device_id=peer, device_id_type=MESH)

    local_in = [
        pltpu.make_async_copy(tp_hbm, tp, lsem.at[0]),
        pltpu.make_async_copy(sp_hbm, sp, lsem.at[1]),
        pltpu.make_async_copy(u_hbm, u, lsem.at[2]),
        pltpu.make_async_copy(vown, vbuf.at[:, pl.ds(pl.multiple_of(t * chunk, chunk), chunk)], lsem.at[3]),
        pltpu.make_async_copy(coeff_hbm, coeff, lsem.at[4]),
        pltpu.make_async_copy(tc_hbm, tc_ref, lsem.at[5]),
        pltpu.make_async_copy(sc_hbm, sc_ref, lsem.at[6]),
    ]
    for copy in local_in:
        copy.start()
    pl.semaphore_wait(barrier, len(HOPS) + 4)

    def own_rows(who, j):
        return vbuf.at[j, pl.ds(pl.multiple_of(who * chunk, chunk), chunk)]

    def direct(j, d):
        return pltpu.make_async_remote_copy(
            src_ref=vown.at[j], dst_ref=own_rows(t, j), send_sem=vsend, recv_sem=vdir.at[j, d],
            device_id=ypeers[d], device_id_type=MESH)

    def to_partner(j, who, src):
        return pltpu.make_async_remote_copy(
            src_ref=src, dst_ref=own_rows(who, j), send_sem=vsend, recv_sem=vpart.at[j],
            device_id=partner, device_id_type=MESH)

    def strip(ref, q):
        return ref.at[:, pl.ds(PARTS[q][0] * 128, PARTS[q][1] * 128)]

    for q in range(len(PARTS)):
        for d in range(3):
            pltpu.make_async_remote_copy(
                src_ref=strip(vown.at[0], q), dst_ref=strip(own_rows(t, 0), q), send_sem=vsend,
                recv_sem=sdir.at[q, d], device_id=ypeers[d], device_id_type=MESH).start()
        pltpu.make_async_remote_copy(
            src_ref=strip(vown.at[0], q), dst_ref=strip(own_rows(t, 0), q), send_sem=vsend,
            recv_sem=spart.at[q], device_id=partner, device_id_type=MESH).start()

    def forward_strip(q):
        for d, back in ((0, 3), (1, 1), (2, 2)):
            who = ((y + back) % RING) * 2 + c
            piece = strip(own_rows(who, 0), q)
            pltpu.make_async_copy(piece, piece, sdir.at[q, d]).wait()
            pltpu.make_async_remote_copy(
                src_ref=piece, dst_ref=piece, send_sem=vsend,
                recv_sem=spart.at[q], device_id=partner, device_id_type=MESH).start()

    def forward(j):
        for d, back in ((0, 3), (1, 1), (2, 2)):
            who = ((y + back) % RING) * 2 + c
            pltpu.make_async_copy(own_rows(who, j), own_rows(who, j), vdir.at[j, d]).wait()
            to_partner(j, who, own_rows(who, j)).start()

    local_in[0].wait()
    local_in[1].wait()
    for i in range(ni):
        xyz = [tp[comp, i : i + 1] - 0.5 for comp in range(3)]
        norm = xyz[0] * xyz[0] + xyz[1] * xyz[1] + xyz[2] * xyz[2] + softening
        cols = jnp.concatenate([-2.0 * p for p in xyz] + [norm, jnp.zeros((4, npts), F32)], axis=0).T
        for comp in range(4):
            tcol[i, comp] = jnp.broadcast_to(cols[:, comp : comp + 1], (npts, 128))
    for j in range(nj):
        xyz = [sp[comp, j : j + 1] - 0.5 for comp in range(3)]
        norm = xyz[0] * xyz[0] + xyz[1] * xyz[1] + xyz[2] * xyz[2]
        for comp, line in enumerate(xyz + [norm]):
            srow[j, comp : comp + 1] = line
    def strip_of_k(j, i, part, q):
        lanes = pl.ds(q * 128, 128)
        tc = [tcol[i, comp, part] for comp in range(4)]
        sr = [srow[j, comp : comp + 1, lanes] for comp in range(4)]
        total = (tc[3] + sr[3]) + tc[0] * sr[0] + tc[1] * sr[1] + tc[2] * sr[2]
        return lax.rsqrt(total).astype(BF16)

    def masked(j, i, tile, first):
        row_id = lax.broadcasted_iota(jnp.int32, tile.shape, 0)
        col_id = lax.broadcasted_iota(jnp.int32, tile.shape, 1) + first
        keep = (row_id < tc_ref[i]) & (col_id < sc_ref[j])
        return jnp.where(keep, tile, 0.0).astype(BF16)

    def basis(i):
        return jnp.concatenate([ut[i, q] for q in range(wide)], axis=1)

    def send_rows(j, i, strips):
        slot = j * ni + i

        def rows_of(who):
            return tiles.at[slot, strips, pl.ds(pl.multiple_of(who * rows, 8), rows)]

        for hop in HOPS:
            peer = src_peer(hop)
            pltpu.make_async_remote_copy(
                src_ref=rows_of(peer), dst_ref=stage.at[s, i, j, strips], send_sem=ssem, recv_sem=rsem.at[j],
                device_id={"src": peer}, device_id_type=MESH).start()
        pltpu.make_async_copy(rows_of(s), stage.at[s, i, j, strips], osem.at[j]).start()

    def pair(j, i):
        step = 512
        for first in range(0, npts, step):
            part = pl.ds(first, step)
            kern = jnp.concatenate([strip_of_k(j, i, part, q) for q in range(wide)], axis=1)
            piece = jnp.dot(kern, vbuf[j], preferred_element_type=F32).astype(BF16)
            for q in range(nstrip):
                half[q, part] = piece[:, q * 128 : (q + 1) * 128]
        right = jnp.concatenate([half[q] for q in range(nstrip)], axis=1)
        tile = masked(j, i, jnp.dot(basis(i), right, preferred_element_type=F32), 0)
        for q in range(nstrip):
            tiles[j * ni + i, q] = tile[:, q * 128 : (q + 1) * 128]
        acc[i] += jnp.dot(tile, coeff[j], preferred_element_type=F32)

    every = pl.ds(0, nstrip)

    def k_whole(i):
        for first in range(0, npts, 256):
            part = pl.ds(first, 256)
            for q in range(wide):
                kbuf[i, q, part] = strip_of_k(0, i, part, q)

    k_whole(0)
    forward_strip(0)

    def gather(j):
        for d in range(3):
            direct(j, d).start()
        to_partner(j, t, vown.at[j]).start()

    for j in range(1, 1 + AHEAD):
        gather(j)
    local_in[2].wait()
    for i in range(ni):
        for q in range(wide):
            ut[i, q] = u[i, q * 128 : (q + 1) * 128].T
    for copy in local_in[3:]:
        copy.wait()
    for n, (strip0, count) in enumerate(PARTS):
        lanes = pl.ds(strip0 * 128, count * 128)
        seen = vbuf.at[0, pl.ds(0, 4 * chunk), lanes]
        pltpu.make_async_copy(seen, seen, spart.at[n]).wait()
        for i in range(ni):
            if n == 0 and i > 0:
                k_whole(i)
            kern = jnp.concatenate([kbuf[i, p] for p in range(wide)], axis=1)
            right = jnp.dot(kern, vbuf[0, :, lanes], preferred_element_type=F32).astype(BF16)
            tile = masked(0, i, jnp.dot(basis(i), right, preferred_element_type=F32), strip0 * 128)
            for q in range(count):
                tiles[i, strip0 + q] = tile[:, q * 128 : (q + 1) * 128]
            send_rows(0, i, pl.ds(strip0, count))
            if n + 1 < len(PARTS) and i == 0:
                forward_strip(n + 1)
    forward(1)
    for i in range(ni):
        tile = jnp.concatenate([tiles[i, q] for q in range(nstrip)], axis=1)
        acc[i] = jnp.dot(tile, coeff[0], preferred_element_type=F32)

    def drain(ref, sem):
        pltpu.make_async_copy(ref, ref, sem).wait()

    def mix(j):
        drain(stage.at[pl.ds(0, others), :, j], rsem.at[j])
        drain(stage.at[0, :, j], osem.at[j])

        @pl.loop(0, nsrc)
        def _(who):
            for i in range(ni):
                for q in range(nstrip):
                    line = stage[who, i, j, q].astype(F32)
                    mixed[i, who, q, pl.ds(j, rows, stride=nj)] = line

    @pl.loop(1, nj)
    def _(j):
        @pl.when(j + AHEAD < nj)
        def _():
            gather(j + AHEAD)

        whole = vbuf.at[j, pl.ds(0, 4 * chunk)]
        pltpu.make_async_copy(whole, whole, vpart.at[j]).wait()
        pair(j, 0)

        @pl.when(j + 1 < nj)
        def _():
            send_rows(j, 0, every)
            forward(j + 1)

        pair(j, 1)

        @pl.when(j + 1 < nj)
        def _():
            send_rows(j, 1, every)

        @pl.when(j >= LAG)
        def _():
            mix(j - LAG)

    def hop_of(i, d):
        return (d, 0) if i == 0 else (0, d)

    def place(ref, i, d):
        to = (z + d) % RING if i == 0 else (x + d) % RING
        return ref.at[i, to] if i == 0 else ref.at[i, :, to]

    for i in range(ni):
        accb[i] = acc[i].astype(BF16).reshape(accb.shape[1:])
    mine = [z, x]
    for d in (1, 3, 2):
        for i in range(ni):
            pltpu.make_async_remote_copy(
                src_ref=place(accb, i, d), dst_ref=part1.at[i, RING - d], send_sem=psend.at[0], recv_sem=precv.at[0],
                device_id={"src": src_peer(hop_of(i, d))}, device_id_type=MESH).start()
    for i in range(ni):
        send_rows(nj - 1, i, every)

    @pl.loop(nj - LAG, nj - 1)
    def _(j):
        mix(j)

    drain(part1.at[:, pl.ds(1, RING - 1)], precv.at[0])
    for i in range(ni):
        own = accb[0, z] if i == 0 else accb[1, :, x]
        total = own.astype(F32)
        for d in range(1, RING):
            total = total + part1[i, d].astype(F32)
        psum[i] = total.astype(BF16)
        other = mine[1 - i]
        pstage[i, 0] = psum[i, other]
        for d in (1, 3, 2):
            pltpu.make_async_remote_copy(
                src_ref=psum.at[i, (other + d) % RING], dst_ref=pstage.at[i, RING - d], send_sem=psend.at[1],
                recv_sem=precv.at[1], device_id={"src": src_peer(hop_of(1 - i, d))}, device_id_type=MESH).start()
    mix(nj - 1)
    drain(pstage.at[:, pl.ds(1, RING - 1)], precv.at[1])
    drain(part1.at[:, pl.ds(1, RING - 1)], psend.at[0])
    drain(pstage.at[:, pl.ds(1, RING - 1)], psend.at[1])
    for _ in range(ni):
        drain(stage.at[pl.ds(0, others), 0], ssem)
    for _ in range(7):
        drain(vown, vsend)


def spread(mixed, pstage, reduced, projected):
    _, nsrc, nstrip, _, lanes = mixed.shape
    band = reduced.shape[1]
    nj = reduced.shape[2] // nsrc
    at = pl.ds(pl.multiple_of(pl.program_id(1) * band * nj, band * nj), band * nj)
    for who in range(nsrc):
        for q in range(nstrip):
            block = mixed[pl.program_id(0), who, q, at].reshape(band, nj, lanes)
            reduced[0, :, who * nj : (who + 1) * nj, q * lanes : (q + 1) * lanes] = block.astype(BF16)

    @pl.when((pl.program_id(0) == 0) & (pl.program_id(1) == 0))
    def _():
        total = jnp.zeros(projected.shape, F32)
        for who in range(pstage.shape[1]):
            total = total + pstage[:, who].astype(F32)
        projected[...] = total.astype(BF16)


def body(
    test_points, test_basis, test_counts, source_points, source_basis, source_counts, coefficients
):
    ni, npts, kmax = test_basis.shape
    nj = source_points.shape[0]
    ncol = coefficients.shape[2]
    nsrc = lax.axis_size("src")
    rows = kmax // nsrc
    vmem = pl.BlockSpec(memory_space=pltpu.VMEM)
    smem = pl.BlockSpec(memory_space=pltpu.SMEM)
    hbm = pl.BlockSpec(memory_space=pltpu.HBM)
    dma = pltpu.SemaphoreType.DMA
    mixed, pstage = pl.pallas_call(
        fused,
        out_shape=(
            pltpu.VMEM((ni, nsrc, kmax // 128, rows * nj, 128), F32),
            pltpu.VMEM((ni, RING, rows, ncol), BF16),
        ),
        in_specs=[hbm, hbm, hbm, hbm, hbm, hbm, hbm],
        out_specs=(vmem, vmem),
        scratch_shapes=[
            pltpu.VMEM((nsrc, ni, nj, kmax // 128, rows, 128), BF16),
            pltpu.VMEM((nj, npts, kmax), BF16),
            pltpu.VMEM((nj * ni, kmax // 128, kmax, 128), BF16),
            pltpu.VMEM((ni, kmax, ncol), F32),
            pltpu.VMEM((ni, RING, RING, rows, ncol), BF16),
            pltpu.VMEM((ni, RING, RING, rows, ncol), BF16),
            pltpu.VMEM((ni, RING, rows, ncol), BF16),
            pltpu.VMEM((ni, npts // 128, npts, 128), BF16),
            pltpu.VMEM((ni, 4, npts, 128), F32),
            pltpu.VMEM((nj, 4, npts), F32),
            pltpu.VMEM((kmax // 128, npts, 128), BF16),
            pltpu.SMEM((ni,), jnp.int32),
            pltpu.SMEM((nj,), jnp.int32),
            pltpu.VMEM((3, ni, npts), F32),
            pltpu.VMEM((3, nj, npts), F32),
            pltpu.VMEM((ni, npts, kmax), BF16),
            pltpu.VMEM((ni, npts // 128, kmax, 128), BF16),
            pltpu.VMEM((nj, kmax, ncol), BF16),
            dma, dma((nj,)), dma((2,)), dma((2,)), dma, dma((nj, 3)), dma((nj,)), dma((7,)), dma((nj,)),
            dma((kmax // 128, 3)), dma((kmax // 128,)),
        ],
        compiler_params=pltpu.CompilerParams(
            collective_id=0, has_side_effects=True, vmem_limit_bytes=67043328 - 9633792
        ),
        name="fused",
    )(
        test_counts, source_counts,
        jnp.transpose(test_points, (1, 0, 2)), jnp.transpose(source_points, (1, 0, 2)),
        test_basis, coefficients, source_basis,
    )
    band = 8
    reduced, projected = pl.pallas_call(
        spread,
        grid=(ni, rows // band),
        out_shape=(
            jax.ShapeDtypeStruct((ni, rows, nsrc * nj, kmax), BF16),
            jax.ShapeDtypeStruct((ni, rows, ncol), BF16),
        ),
        in_specs=[vmem, vmem],
        out_specs=(
            pl.BlockSpec((1, band, nsrc * nj, kmax), lambda i, r: (i, r, 0, 0)),
            pl.BlockSpec((ni, rows, ncol), lambda i, r: (0, 0, 0)),
        ),
        compiler_params=pltpu.CompilerParams(vmem_limit_bytes=16 * 1024 * 1024),
        name="spread",
    )(
        pltpu.with_memory_space_constraint(mixed, pltpu.VMEM),
        pltpu.with_memory_space_constraint(pstage, pltpu.VMEM),
    )
    return (reduced, projected)


def solution(mesh):
    return jax.shard_map(
        body,
        mesh=mesh,
        in_specs=(
            P("test", None, None),
            P("test", None, None),
            P("test"),
            P("src", None, None),
            P("src", "test", None),
            P("src"),
            P("src", None, None),
        ),
        out_specs=(P("test", "src", None, None), P("test", "src", None)),
        check_vma=False,
    )
```
